256 devices in a mesh: seq: 64 (over x, z, core), tp: 4 (over y).
Axes of the slice: x: 4, y: 4, z: 8, core: 2. Of those that a mesh axis runs over, the one named last changes fastest.
Arguments:
- queries: bfloat16 [65536, 2048], P('seq', 'tp'), may hold values from -6.5 to 6.5
- db_keys: bfloat16 [1024, 128, 2048], P('seq', None, 'tp'), may hold values from -6 to 6
- db_values: bfloat16 [1024, 128, 2048], P('seq', None, 'tp'), may hold values from -12 to 12
- nb_shard: int32 [1024, 2], P('seq'), may hold values from 0 to 63, all different within a row; in each aligned block of 16 rows (0 to 15, 16 to 31, ...) at most 2 rows name the same one
- nb_row: int32 [1024, 2], P('seq'), may hold values from 0 to 15
- out_weight: bfloat16 [2048, 4096], P('seq', 'tp'), may hold values from -0.125 to 0.125
Outputs:
- mixed: bfloat16 [65536, 4096], P('seq', 'tp')
The draws below stay inside these ranges and needn't reach their ends.
Inputs may be any that keep to these rules, and one draw needn't show every extreme that they name: `nb_shard`: among the 16 blocks of one index of seq no shard is named more than 2 times, a bound that some block reaches in some such group; the 2 shards of one block differ.
All inputs are finite; a program needn't handle non-finite values.
Results may differ from the reference program's by a relative error of at most 0.024.
Values may be sent and summed in bfloat16 or wider, within the bound.
No kernel may reach another device: no remote copies, remote signals or barrier semaphores. Data moves between devices by JAX's collectives and lax.ppermute only.
A program may use at most 192 MiB of HBM per device.

```python
import math
import jax
import jax.numpy as jnp
import numpy as np
from jax import lax

D = 4096
HD = 128
BLOCK = 64
NBR = 2
NLEN = 128
TOK_DEV = 1024
DB_DEV = 16
HQ = 2048
BLOCKS_DEV = 16
CAP = 2
TOKENS = 65536
NBLOCKS = 1024
DB_ROWS = 1024
N_SEQ = 64
N_TP = 4


def draw_queries(key, part):
    drawn = jnp.clip(jax.random.normal(jax.random.fold_in(key, 11), (TOKENS, HQ), jnp.float32), -4.0, 4.0)
    return drawn.astype(jnp.bfloat16)


def draw_db_keys(key, part):
    drawn = 1.5 * jnp.clip(jax.random.normal(jax.random.fold_in(key, 23), (DB_ROWS, NLEN, HQ), jnp.float32), -4.0, 4.0)
    return drawn.astype(jnp.bfloat16)


def with_ends(result, stream_key, smallest, top_value):
    dims = result.shape
    index_at = [jax.random.randint(jax.random.fold_in(stream_key, axis), (), 0, dims[axis]) for axis in range(len(dims))]
    result = result.at[tuple(index_at)].set(smallest)
    longest = dims.index(max(dims))
    index_at[longest] = (index_at[longest] + 1) % dims[longest]
    return result.at[tuple(index_at)].set(top_value)


def levels(rng, shape, cuts, smallest, high):
    loudness, own = 1.0, jax.random.fold_in(rng, 6)
    for position, blocks in cuts:
        draws = jnp.exp(jax.random.uniform(jax.random.fold_in(own, position), (blocks,), jnp.float32, smallest / len(cuts), high / len(cuts)))
        loudness = loudness * jnp.repeat(draws, shape[position] // blocks).reshape([-1 if axis == position else 1 for axis in range(len(shape))])
    return loudness


def cumulative_ranks(number_of, skew):
    portions = [(1 << 20) // math.isqrt(standing ** skew) + 1 for standing in range(1, number_of + 1)]
    width = 1 + sum(portions) // (1 << 30)
    return np.cumsum(np.array([max(1, weight // width) for weight in portions]))


def ranked_ids(rng, dims, number_of, lean):
    listing = cumulative_ranks(number_of, lean)
    lot = jax.random.randint(jax.random.fold_in(rng, 1), dims, 0, int(listing[number_of - 1]))
    rank = jnp.searchsorted(jnp.asarray(listing, jnp.int32), lot, side="right")
    return jax.random.permutation(jax.random.fold_in(rng, 2), number_of)[rank].astype(jnp.int32)


def deal_out(own_key, own, number, rows, number_of, top, bound, lean):
    order = jax.random.permutation(own_key, number_of)
    packed, usual = load_shares(number_of, rows * top, bound, lean, True), load_shares(number_of, rows * top, bound, lean, False)
    places = jnp.arange(number_of)

    def named(lengths, offset_by):
        used = int((lengths > 0).sum())
        fixed = max(1, used // 4)
        moved = fixed + (places - fixed + offset_by * (used - fixed)) % max(1, number_of - fixed)
        return jnp.zeros((number_of,), jnp.int32).at[order[jnp.where(places < fixed, places, moved)]].set(jnp.asarray(lengths, jnp.int32))

    lengths = jnp.where(number % 4 == 0, named(packed, number // 4), named(usual, number - number // 4 - 1))
    mixed = jax.random.permutation(jax.random.fold_in(own, 3), number_of)
    giver, sink = mixed[0:number_of // 2 * 2:2], mixed[1:number_of // 2 * 2:2]
    room = jnp.minimum(lengths[giver] - 1, bound - lengths[sink]) // 2
    room = jnp.where((giver == order[0]) | (sink == order[0]) | (lengths[sink] == 0), 0, jnp.maximum(room, 0))
    moved = jax.random.randint(jax.random.fold_in(own, 4), (number_of // 2,), 0, 1 << 20) % (room + 1)
    lengths = lengths.at[giver].add(-moved).at[sink].add(moved)
    items = jnp.searchsorted(jnp.cumsum(lengths), jnp.arange(rows * top), side="right").astype(jnp.int32)
    listing = items.reshape(top, rows).T
    listing = listing[jax.random.permutation(jax.random.fold_in(own, 1), rows)]
    offset_by = jax.random.randint(jax.random.fold_in(own, 2), (rows, 1), 0, top)
    return jnp.take_along_axis(listing, (jnp.arange(top)[None, :] + offset_by) % top, axis=1)


def load_shares(count, total, limit, lean, full):
    portions = [(1 << 20) // math.isqrt(grade ** lean) + 1 for grade in range(1, count + 1)]
    largest = limit if full else min(limit, max(-(-total // count), total * portions[0] // sum(portions)))
    least = 1 if total - largest >= count - 1 else 0
    counts, surplus = [largest] + [least] * (count - 1), total - largest - least * (count - 1)
    while surplus > 0:
        movable = [i for i in range(1, count) if counts[i] < largest] or [i for i in range(1, count) if counts[i] < limit]
        whole, remaining = sum([portions[i] for i in movable]), surplus
        for i in movable:
            addition = min(limit - counts[i], max(1, remaining * portions[i] // whole), surplus)
            counts[i] = counts[i] + addition
            surplus = surplus - addition
    return np.array(counts)


def noise(own_key, extent, deviation, bound, cuts=(), held_as=jnp.bfloat16):
    values = deviation * jax.random.normal(own_key, extent, jnp.float32)
    if cuts:
        values = values * levels(own_key, extent, cuts, -0.22, 0.18)
    return jnp.clip(values, -bound, bound).astype(held_as)


def setup_inputs(seed: int = 0) -> dict:
    arg_keys = jax.random.split(jax.random.key(seed), 7)
    queries = draw_queries(jax.random.fold_in(arg_keys[6], 71), 0)
    db_keys = draw_db_keys(jax.random.fold_in(arg_keys[6], 71), 0)
    db_values = noise(arg_keys[2], (DB_ROWS, NLEN, HQ), 3.0, 12.0, ((0, 64), (2, 4)))
    nb_shard_keys = jax.random.split(jax.random.fold_in(arg_keys[3], 1), NBLOCKS // BLOCKS_DEV)
    nb_shard_turns = jax.random.permutation(jax.random.fold_in(arg_keys[3], 3), NBLOCKS // BLOCKS_DEV)
    nb_shard = jax.vmap(lambda own, number: deal_out(jax.random.fold_in(arg_keys[3], 2), own, number, BLOCKS_DEV, N_SEQ, NBR, CAP, 2))(nb_shard_keys, nb_shard_turns).reshape((NBLOCKS, NBR))
    nb_row = with_ends(ranked_ids(arg_keys[4], (NBLOCKS, NBR), DB_DEV, 2), jax.random.fold_in(arg_keys[4], 3), 0, DB_DEV - 1).astype(jnp.int32)
    out_weight = noise(arg_keys[5], (HQ, D), HQ ** -0.5, 0.125, ((0, 64), (1, 4)))
    return dict(queries=queries, db_keys=db_keys, db_values=db_values, nb_shard=nb_shard, nb_row=nb_row, out_weight=out_weight)


def reference(queries, db_keys, db_values, nb_shard, nb_row, out_weight):
    score_scale = float(HD) ** -0.5
    tokens = queries.shape[0]
    feature_cols = queries.shape[1]
    heads_all = feature_cols // HD
    shifted = jnp.concatenate([queries[BLOCK - 1:], jnp.zeros((BLOCK - 1, feature_cols), queries.dtype)], axis=0)
    shifted = shifted.reshape(N_SEQ, BLOCKS_DEV, BLOCK, heads_all, HD)
    entry_index = (nb_shard * DB_DEV + nb_row).astype(jnp.int32).reshape(N_SEQ, BLOCKS_DEV, NBR)

    def attend_block(block_args):
        query_block, index_block = block_args
        key_rows = db_keys[index_block].astype(jnp.float32).reshape(BLOCKS_DEV, NBR, NLEN, heads_all, HD)
        value_rows = db_values[index_block].astype(jnp.float32).reshape(BLOCKS_DEV, NBR, NLEN, heads_all, HD)
        scores = jnp.einsum("bqhd,bnkhd->bnhqk", query_block.astype(jnp.float32), key_rows) * score_scale
        row_max = jnp.max(scores, axis=-1, keepdims=True)
        log_total = row_max[..., 0] + jnp.log(jnp.sum(jnp.exp(scores - row_max), axis=-1))
        weights = jnp.exp(scores - log_total[..., None]).astype(jnp.bfloat16)
        partial_value = jnp.einsum("bnhqk,bnkhd->bnqhd", weights.astype(jnp.float32), value_rows).astype(jnp.bfloat16)
        best_log = jnp.max(log_total, axis=1, keepdims=True)
        merged_log = best_log + jnp.log(jnp.sum(jnp.exp(log_total - best_log), axis=1, keepdims=True))
        share = jnp.transpose(jnp.exp(log_total - merged_log), (0, 1, 3, 2))[..., None]
        attended = jnp.sum(share * partial_value.astype(jnp.float32), axis=1).astype(jnp.bfloat16)
        return attended.reshape(BLOCKS_DEV * BLOCK, feature_cols)

    attended = lax.map(attend_block, (shifted, entry_index)).reshape(tokens, feature_cols)
    placed = jnp.concatenate([jnp.zeros((BLOCK - 1, feature_cols), jnp.bfloat16), attended[:tokens - (BLOCK - 1)]], axis=0)
    group_cols = feature_cols // N_TP

    def project_rows(row_block):
        summed = jnp.zeros((row_block.shape[0], out_weight.shape[1]), jnp.float32)
        for group in range(N_TP):
            product = jnp.dot(row_block[:, group * group_cols:(group + 1) * group_cols], out_weight[group * group_cols:(group + 1) * group_cols], preferred_element_type=jnp.float32)
            rounded = lax.optimization_barrier(product.astype(jnp.bfloat16))
            summed = summed + rounded.astype(jnp.float32)
        return summed.astype(jnp.bfloat16)

    mixed = lax.map(project_rows, placed.reshape(N_SEQ, TOK_DEV, feature_cols))
    return mixed.reshape(tokens, out_weight.shape[1])
```

```python
import jax
import jax.numpy as jnp
from jax import lax
from jax.experimental import pallas as pl
from jax.experimental.pallas import tpu as pltpu
from jax.sharding import PartitionSpec as P

HD = 128
BLOCK = 64
NBR = 2
NLEN = 128
PAIR = 2 * HD
SLOTS_STEP = 8


def from_behind(shard, axis, by):
    count = lax.axis_size(axis)
    pairs = [(i, i + by) for i in range(count) if 0 <= i + by < count]
    return lax.ppermute(shard, axis, pairs)


def attend_body(rows_ref, q_ref, k_ref, v_ref, out_ref, log_ref):
    step = pl.program_id(0)
    first_head = lax.broadcasted_iota(jnp.int32, (NLEN, 2 * BLOCK), 1) < BLOCK
    nt = (((1,), (1,)), ((), ()))
    for j in range(SLOTS_STEP):
        row = rows_ref[step * SLOTS_STEP + j]
        q2 = jnp.concatenate([q_ref[j, :, :HD], q_ref[j, :, HD:]], axis=0)
        s0 = lax.dot_general(k_ref[row, :, :HD], q2, nt, preferred_element_type=jnp.float32)
        s1 = lax.dot_general(k_ref[row, :, HD:], q2, nt, preferred_element_type=jnp.float32)
        s = jnp.where(first_head, s0, s1) * (float(HD) ** -0.5)
        top = jnp.max(s, axis=0, keepdims=True)
        e = jnp.exp(s - top)
        total = jnp.sum(e, axis=0, keepdims=True)
        log_ref[pl.ds(j, 1), :] = top + jnp.log(total)
        w = jnp.transpose(e * (1.0 / total)).astype(jnp.bfloat16)
        out_ref[j, :, :HD] = jnp.dot(
            w[:BLOCK], v_ref[row, :, :HD], preferred_element_type=jnp.float32
        ).astype(jnp.bfloat16)
        out_ref[j, :, HD:] = jnp.dot(
            w[BLOCK:], v_ref[row, :, HD:], preferred_element_type=jnp.float32
        ).astype(jnp.bfloat16)


def attend(rows, q, k, v, chunk):
    slots = q.shape[0]
    entries = k.shape[0]
    return pl.pallas_call(
        attend_body,
        grid_spec=pltpu.PrefetchScalarGridSpec(
            num_scalar_prefetch=1,
            grid=(slots // SLOTS_STEP,),
            in_specs=[
                pl.BlockSpec((SLOTS_STEP, BLOCK, PAIR), lambda i, r: (i, 0, 0)),
                pl.BlockSpec((entries, NLEN, PAIR), lambda i, r: (0, 0, chunk)),
                pl.BlockSpec((entries, NLEN, PAIR), lambda i, r: (0, 0, chunk)),
            ],
            out_specs=[
                pl.BlockSpec((SLOTS_STEP, BLOCK, PAIR), lambda i, r: (i, 0, 0)),
                pl.BlockSpec((SLOTS_STEP, 2 * BLOCK), lambda i, r: (i, 0)),
            ],
        ),
        out_shape=[
            jax.ShapeDtypeStruct((slots, BLOCK, PAIR), jnp.bfloat16),
            jax.ShapeDtypeStruct((slots, 2 * BLOCK), jnp.float32),
        ],
        name="attend",
    )(rows, q, k, v)


def merge_body(slot_ref, first_ref, second_ref, log_ref, out_ref):
    u = pl.program_id(0)
    l0 = log_ref[pl.ds(slot_ref[2 * u], 1), :]
    l1 = log_ref[pl.ds(slot_ref[2 * u + 1], 1), :]
    best = jnp.maximum(l0, l1)
    e0 = jnp.exp(l0 - best)
    e1 = jnp.exp(l1 - best)
    inv = 1.0 / (e0 + e1)
    side = 2 * BLOCK
    c0 = jnp.transpose(jnp.broadcast_to(e0 * inv, (side, side)))
    c1 = jnp.transpose(jnp.broadcast_to(e1 * inv, (side, side)))
    p0 = first_ref[0].astype(jnp.float32)
    p1 = second_ref[0].astype(jnp.float32)
    out_ref[:, :HD] = (c0[:BLOCK] * p0[:, :HD] + c1[:BLOCK] * p1[:, :HD]).astype(jnp.bfloat16)
    out_ref[:, HD:] = (c0[BLOCK:] * p0[:, HD:] + c1[BLOCK:] * p1[:, HD:]).astype(jnp.bfloat16)


def merge(slot_index, partials, logs):
    blocks = slot_index.shape[0] // NBR
    slots = partials.shape[0]
    return pl.pallas_call(
        merge_body,
        grid_spec=pltpu.PrefetchScalarGridSpec(
            num_scalar_prefetch=1,
            grid=(blocks,),
            in_specs=[
                pl.BlockSpec((1, BLOCK, PAIR), lambda u, s: (s[2 * u], 0, 0)),
                pl.BlockSpec((1, BLOCK, PAIR), lambda u, s: (s[2 * u + 1], 0, 0)),
                pl.BlockSpec((slots, 2 * BLOCK), lambda u, s: (0, 0)),
            ],
            out_specs=pl.BlockSpec((BLOCK, PAIR), lambda u, s: (u, 0)),
        ),
        out_shape=jax.ShapeDtypeStruct((blocks * BLOCK, PAIR), jnp.bfloat16),
        name="merge",
    )(slot_index, partials, partials, logs)


def per_device(queries, db_keys, db_values, nb_shard, nb_row, out_weight):
    tok_rows = queries.shape[0]
    feature_cols = queries.shape[1]
    chunks = feature_cols // PAIR
    blocks = tok_rows // BLOCK
    shards = lax.axis_size("seq")
    groups = lax.axis_size("tp")
    capacity = max(2, 4 * blocks // shards)
    slots = shards * capacity
    upcoming = from_behind(queries[:BLOCK], "seq", -1)
    owners = nb_shard.reshape(-1)
    entries = nb_row.reshape(-1)
    requests = owners.shape[0]
    positions = jnp.arange(requests, dtype=jnp.int32)
    same_owner = (owners[:, None] == owners[None, :]) & (positions[None, :] < positions[:, None])
    slot_rank = jnp.sum(same_owner.astype(jnp.int32), axis=1)
    slot_index = owners * capacity + slot_rank
    holds = slot_index[None, :] == jnp.arange(slots, dtype=jnp.int32)[:, None]
    wanted = jnp.sum(jnp.where(holds, entries[None, :], 0), axis=1)
    block_of = jnp.sum(jnp.where(holds, (positions // NBR)[None, :], 0), axis=1)
    rows = lax.all_to_all(
        wanted.reshape(shards, capacity), "seq", split_axis=0, concat_axis=0, tiled=True
    ).reshape(-1)
    extended = jnp.concatenate([queries[BLOCK - 1 :], upcoming[: BLOCK - 1]], axis=0).reshape(
        blocks, BLOCK, feature_cols
    )
    asked = []
    for c in range(chunks):
        outgoing = extended[:, :, c * PAIR : (c + 1) * PAIR][block_of]
        asked.append(
            lax.all_to_all(
                outgoing.reshape(shards, capacity, BLOCK, PAIR),
                "seq",
                split_axis=0,
                concat_axis=0,
                tiled=True,
            )
        )
    rows_all = lax.all_gather(out_weight, "seq", axis=0, tiled=True)
    weight = rows_all.reshape(groups, chunks, PAIR, out_weight.shape[1])
    returned = []
    all_logs = []
    for c in range(chunks):
        part, logs = attend(rows, asked[c].reshape(slots, BLOCK, PAIR), db_keys, db_values, c)
        all_logs.append(logs.astype(jnp.bfloat16))
        returned.append(
            lax.all_to_all(
                part.reshape(shards, capacity, BLOCK, PAIR),
                "seq",
                split_axis=0,
                concat_axis=0,
                tiled=True,
            )
        )
    logs_back = lax.all_to_all(
        jnp.concatenate(all_logs, axis=1).reshape(shards, capacity, chunks * 2 * BLOCK),
        "seq",
        split_axis=0,
        concat_axis=0,
        tiled=True,
    ).reshape(slots, chunks * 2 * BLOCK)
    mixed = None
    for c in range(chunks):
        attended = merge(
            slot_index,
            returned[c].reshape(slots, BLOCK, PAIR),
            logs_back[:, c * 2 * BLOCK : (c + 1) * 2 * BLOCK].astype(jnp.float32),
        )
        tail_rows = from_behind(attended[-BLOCK:], "seq", 1)
        placed = jnp.concatenate([tail_rows[1:], attended[: tok_rows - (BLOCK - 1)]], axis=0)
        placed_all = lax.all_gather(placed, "tp", axis=1, tiled=True)
        term = jnp.dot(
            placed_all,
            weight[:, c].reshape(groups * PAIR, -1),
            preferred_element_type=jnp.float32,
        )
        mixed = term if mixed is None else mixed + term
    return mixed.astype(jnp.bfloat16)


def solution(mesh):
    placed = (
        P("seq", "tp"),
        P("seq", None, "tp"),
        P("seq", None, "tp"),
        P("seq", None),
        P("seq", None),
        P("seq", "tp"),
    )
    return jax.shard_map(
        per_device, mesh=mesh, in_specs=placed, out_specs=P("seq", "tp"), check_vma=False
    )
```
